32 devices in a mesh: band: 4 (over z), sector: 8 (over y, x, core).
Axes of the slice: x: 2, y: 2, z: 4, core: 2. Of those that a mesh axis runs over, the one named last changes fastest.
Arguments:
- node_states: bfloat16 [16, 128, 512], P('band', 'sector'), may hold values from -6 to 6
- edge_states: bfloat16 [32, 512, 512], P(('band', 'sector')), may hold values from -6 to 6
- senders: int32 [32, 512], P(('band', 'sector')), may hold values from 0 to 351, as said below
- receivers: int32 [32, 512], P(('band', 'sector')), may hold values from 0 to 63
- edge_count: int32 [32], P(('band', 'sector')), may hold values from 128 to 512, as said below
- edge_hidden: bfloat16 [2, 1536, 512], replicated, may hold values from -0.15625 to 0.15625
- edge_offset: float32 [2, 512], replicated, may hold values from -3 to 3
- edge_output: bfloat16 [2, 512, 512], replicated, may hold values from -0.25 to 0.25
- edge_scale: float32 [2, 512], replicated, may hold values from 0.5 to 1.5
- node_hidden: bfloat16 [2, 1024, 512], replicated, may hold values from -0.1875 to 0.1875
- node_offset: float32 [2, 512], replicated, may hold values from -3 to 3
- node_output: bfloat16 [2, 512, 512], replicated, may hold values from -0.25 to 0.25
- node_scale: float32 [2, 512], replicated, may hold values from 0.5 to 1.5
- output_cotangent: bfloat16 [16, 128, 512], P('band', 'sector'), may hold values from -6 to 6
Outputs:
- node_result: bfloat16 [16, 128, 512], P('band', 'sector')
- node_gradient: float32 [16, 128, 512], P('band', 'sector')
- edge_gradient: float32 [32, 512, 512], P(('band', 'sector'))
- edge_hidden_gradient: float32 [2, 1536, 512], replicated
- edge_offset_gradient: float32 [2, 512], replicated
- edge_output_gradient: float32 [2, 512, 512], replicated
- edge_scale_gradient: float32 [2, 512], replicated
- node_hidden_gradient: float32 [2, 1024, 512], replicated
- node_offset_gradient: float32 [2, 512], replicated
- node_output_gradient: float32 [2, 512, 512], replicated
- node_scale_gradient: float32 [2, 512], replicated
The draws below stay inside these ranges and needn't reach their ends.
Inputs may be any that keep to these rules, and one draw needn't show every extreme that they name: `senders`: an entry below 288 names a cell of the device's extended block (row-major, 12 rows); devices of the first band never name its first 4 rows, devices of the last band never its last 4 rows. An entry 288 + c names coarse node c. `edge_count`: slots at or past a device's count hold no edge. Some device has all 512 slots live.
All inputs are finite; a program needn't handle non-finite values.
Results may differ from the reference program's by a relative error of at most 0.019.
Values may be sent and summed in bfloat16 or wider, within the bound.
No kernel may reach another device: no remote copies, remote signals or barrier semaphores. Data moves between devices by JAX's collectives and lax.ppermute only.
A program may use at most 128 MiB of HBM per device.

```python
import math
import jax
import jax.numpy as jnp
from jax import lax

D = 512
LB = 4
LS = 16
CO = 2
LAYERS = 2
NODE_DEV = 64
EDGE_DEV = 512
EXT = 288
COARSE = 64
NLAT = 16
NLON = 128
NODES = 2048
N_BAND = 4
N_SECTOR = 8
DEVICES = 32


def draw_senders(key, part):
    key_lat, key_lon, key_coarse, key_pick = jax.random.split(jax.random.fold_in(key, 11), 4)
    band_index = (jnp.arange(DEVICES, dtype=jnp.int32) // N_SECTOR)[:, None]
    lowest = jnp.where(band_index == 0, LB, 0).astype(jnp.int32)
    highest = jnp.where(band_index == N_BAND - 1, 2 * LB, 3 * LB).astype(jnp.int32)
    lat_pos = jax.random.randint(key_lat, (DEVICES, EDGE_DEV), lowest, highest, dtype=jnp.int32)
    lon_pos = jax.random.randint(key_lon, (DEVICES, EDGE_DEV), 0, LS + 2 * LB, dtype=jnp.int32)
    fine_index = lat_pos * (LS + 2 * LB) + lon_pos
    coarse_index = EXT + jax.random.randint(key_coarse, (DEVICES, EDGE_DEV), 0, COARSE, dtype=jnp.int32)
    picked = jax.random.randint(key_pick, (DEVICES, EDGE_DEV), 0, 4, dtype=jnp.int32) == 0
    return jnp.where(picked, coarse_index, fine_index).astype(jnp.int32)


def draw_edge_count(key, part):
    key_count, key_full = jax.random.split(jax.random.fold_in(key, 23), 2)
    counts = jax.random.randint(key_count, (DEVICES,), EDGE_DEV // 4, EDGE_DEV + 1, dtype=jnp.int32)
    fullest = jax.random.randint(key_full, (), 0, DEVICES, dtype=jnp.int32)
    return jnp.where(jnp.arange(DEVICES, dtype=jnp.int32) == fullest, EDGE_DEV, counts).astype(jnp.int32)


def place_ends(values, key, low, top_value):
    extent = values.shape
    place = [jax.random.randint(jax.random.fold_in(key, axis), (), 0, extent[axis]) for axis in range(len(extent))]
    values = values.at[tuple(place)].set(low)
    longest = extent.index(max(extent))
    place[longest] = (place[longest] + 1) % extent[longest]
    return values.at[tuple(place)].set(top_value)


def steps_of(own_key, extent, shards, low, high):
    def one(dim, blocks):
        steps = jax.random.uniform(jax.random.fold_in(jax.random.fold_in(own_key, 6), dim), (blocks,), jnp.float32, low / len(shards), high / len(shards))
        return jnp.repeat(jnp.exp(steps), extent[dim] // blocks).reshape((-1,) + (1,) * (len(extent) - dim - 1))

    loudness = one(*shards[0])
    for cut in shards[1:]:
        loudness = loudness * one(*cut)
    return loudness


def scatter_about(own_key, extent, spread, limit, pieces=(), kind=jnp.bfloat16):
    loudness = steps_of(own_key, extent, pieces, -0.22, 0.18) if pieces else 1.0
    values = jax.random.normal(own_key, extent, jnp.float32) * spread * loudness
    return jnp.minimum(jnp.maximum(values, -limit), limit).astype(kind)


def setup_inputs(seed: int = 0) -> dict:
    splits = jax.random.split(jax.random.key(seed), 15)
    node_states = scatter_about(splits[0], (NLAT, NLON, D), 1.0, 6.0, ((0, 4), (1, 8)))
    edge_states = scatter_about(splits[1], (DEVICES, EDGE_DEV, D), 1.0, 6.0, ((0, 32),))
    senders = draw_senders(jax.random.fold_in(splits[14], 71), 0)
    receivers = place_ends(jax.random.randint(splits[3], (DEVICES, EDGE_DEV), 0, NODE_DEV), jax.random.fold_in(splits[3], 1), 0, NODE_DEV - 1).astype(jnp.int32)
    edge_count = draw_edge_count(jax.random.fold_in(splits[14], 71), 0)
    edge_hidden = scatter_about(splits[5], (LAYERS, 3 * D, D), (3 * D) ** -0.5, 0.15625)
    edge_offset = scatter_about(splits[6], (LAYERS, D), 0.5, 3.0, (), jnp.float32)
    edge_output = scatter_about(splits[7], (LAYERS, D, D), D ** -0.5, 0.25)
    edge_scale = jnp.clip(1.0 + 0.1 * jax.random.normal(splits[8], (LAYERS, D), jnp.float32), 0.5, 1.5)
    node_hidden = scatter_about(splits[9], (LAYERS, 2 * D, D), (2 * D) ** -0.5, 0.1875)
    node_offset = scatter_about(splits[10], (LAYERS, D), 0.5, 3.0, (), jnp.float32)
    node_output = scatter_about(splits[11], (LAYERS, D, D), D ** -0.5, 0.25)
    node_scale = jnp.clip(1.0 + 0.1 * jax.random.normal(splits[12], (LAYERS, D), jnp.float32), 0.5, 1.5)
    output_cotangent = scatter_about(splits[13], (NLAT, NLON, D), 1.0, 6.0, ((0, 4), (1, 8)))
    return {"node_states": node_states, "edge_states": edge_states, "senders": senders, "receivers": receivers, "edge_count": edge_count, "edge_hidden": edge_hidden, "edge_offset": edge_offset, "edge_output": edge_output, "edge_scale": edge_scale, "node_hidden": node_hidden, "node_offset": node_offset, "node_output": node_output, "node_scale": node_scale, "output_cotangent": output_cotangent}


epsilon = 1e-05

def mlp_forward(inputs, first_weight, first_bias, second_weight, norm_gain):
    pre_act = jnp.dot(inputs, first_weight, preferred_element_type=jnp.float32) + first_bias
    sigmoid_val = jax.nn.sigmoid(pre_act)
    activated = (pre_act * sigmoid_val).astype(jnp.bfloat16)
    mixed = jnp.dot(activated, second_weight, preferred_element_type=jnp.float32)
    centered = mixed - lax.optimization_barrier(jnp.mean(mixed, axis=-1, keepdims=True))
    inv_std = lax.rsqrt(lax.optimization_barrier(jnp.mean(centered * centered, axis=-1, keepdims=True)) + epsilon)
    normed = centered * inv_std
    return (normed * norm_gain, (inputs, pre_act, sigmoid_val, activated, normed, inv_std))

def mlp_backward(grad_out, saved, first_weight, second_weight, norm_gain):
    inputs, pre_act, sigmoid_val, activated, normed, inv_std = saved
    grad_gain = lax.optimization_barrier(jnp.sum(grad_out * normed, axis=0))
    grad_normed = grad_out * norm_gain
    grad_mixed = inv_std * (grad_normed - lax.optimization_barrier(jnp.mean(grad_normed, axis=-1, keepdims=True)) - normed * lax.optimization_barrier(jnp.mean(grad_normed * normed, axis=-1, keepdims=True)))
    mixed_low = grad_mixed.astype(jnp.bfloat16)
    grad_second = lax.dot_general(activated, mixed_low, (((0,), (0,)), ((), ())), preferred_element_type=jnp.float32)
    grad_act = lax.dot_general(mixed_low, second_weight, (((1,), (1,)), ((), ())), preferred_element_type=jnp.float32)
    grad_pre = grad_act * sigmoid_val * (1.0 + pre_act * (1.0 - sigmoid_val))
    grad_bias = lax.optimization_barrier(jnp.sum(grad_pre, axis=0))
    pre_low = grad_pre.astype(jnp.bfloat16)
    grad_first = lax.dot_general(inputs, pre_low, (((0,), (0,)), ((), ())), preferred_element_type=jnp.float32)
    grad_inputs = lax.dot_general(pre_low, first_weight, (((1,), (1,)), ((), ())), preferred_element_type=jnp.float32)
    return (grad_inputs, (grad_first, grad_bias, grad_second, grad_gain))

def to_devices(grid):
    width = grid.shape[-1]
    return grid.reshape(N_BAND, LB, N_SECTOR, LS, width).transpose(0, 2, 1, 3, 4).reshape(DEVICES, LB * LS, width)

def to_grid(blocks):
    width = blocks.shape[-1]
    return blocks.reshape(N_BAND, N_SECTOR, LB, LS, width).transpose(0, 2, 1, 3, 4).reshape(NLAT, NLON, width)

def tables_of(state):
    padded = jnp.pad(state, ((LB, LB), (LB, LB), (0, 0)), mode='wrap')
    device_index = jnp.arange(DEVICES, dtype=jnp.int32)
    band_index = device_index // N_SECTOR
    sector_index = device_index % N_SECTOR

    def cut_block(band_pos, sector_pos):
        start = (band_pos * LB, sector_pos * LS, jnp.int32(0))
        return lax.dynamic_slice(padded, start, (3 * LB, LS + 2 * LB, D)).reshape(EXT, D)
    extended = jax.vmap(cut_block)(band_index, sector_index)
    coarse = state.reshape(N_BAND, LB, N_SECTOR, LS, D)[:, 0, :, :CO, :].reshape(COARSE, D)
    return jnp.concatenate([extended, jnp.broadcast_to(coarse, (DEVICES, COARSE, D))], axis=1)

def fold_blocks(blocks):
    blocks = blocks.reshape(DEVICES, 3 * LB, LS + 2 * LB, D)
    padded = jnp.zeros((NLAT + 2 * LB, NLON + 2 * LB, D), jnp.float32)

    def add_block(device_index, accum):
        device_index = device_index.astype(jnp.int32)
        start = (device_index // N_SECTOR * LB, device_index % N_SECTOR * LS, jnp.int32(0))
        current = lax.dynamic_slice(accum, start, (3 * LB, LS + 2 * LB, D))
        return lax.dynamic_update_slice(accum, current + blocks[device_index], start)
    padded = lax.fori_loop(jnp.int32(0), jnp.int32(DEVICES), add_block, padded)
    lon_folded = padded[:, LB:LB + NLON]
    lon_folded = lon_folded.at[:, NLON - LB:].add(padded[:, :LB]).at[:, :LB].add(padded[:, LB + NLON:])
    folded = lon_folded[LB:LB + NLAT]
    folded = folded.at[NLAT - LB:].add(lon_folded[:LB]).at[:LB].add(lon_folded[LB + NLAT:])
    return folded

def coarse_into_grid(coarse_grad):
    canvas = jnp.zeros((N_BAND, LB, N_SECTOR, LS, D), jnp.float32)
    canvas = canvas.at[:, 0, :, :CO].set(coarse_grad.reshape(N_BAND, N_SECTOR, CO, D))
    return canvas.reshape(NLAT, NLON, D)

def reference(node_states, edge_states, senders, receivers, edge_count, edge_hidden, edge_offset, edge_output, edge_scale, node_hidden, node_offset, node_output, node_scale, output_cotangent):
    live_mask = (jnp.arange(EDGE_DEV, dtype=jnp.int32)[None, :] < edge_count[:, None]).astype(jnp.float32)[:, :, None]
    device_index = jnp.arange(DEVICES, dtype=jnp.int32)[:, None]
    recv_ids = (device_index * NODE_DEV + receivers).reshape(-1)
    send_ids = (device_index * (EXT + COARSE) + senders).reshape(-1)
    state = node_states
    edge_rows = edge_states
    records = []
    for depth_index in range(LAYERS):
        tables = tables_of(state)
        own_rows = to_devices(state)
        sent = jnp.take_along_axis(tables, senders[:, :, None], axis=1)
        received = jnp.take_along_axis(own_rows, receivers[:, :, None], axis=1)
        inputs = jnp.concatenate([edge_rows, sent, received], axis=2).reshape(DEVICES * EDGE_DEV, 3 * D)
        result, edge_saved = mlp_forward(inputs, edge_hidden[depth_index], edge_offset[depth_index], edge_output[depth_index], edge_scale[depth_index])
        update = result.reshape(DEVICES, EDGE_DEV, D) * live_mask
        edge_rows = (edge_rows.astype(jnp.float32) + update).astype(jnp.bfloat16)
        summed = jax.ops.segment_sum(update.reshape(-1, D), recv_ids, num_segments=DEVICES * NODE_DEV)
        flat_rows = own_rows.reshape(-1, D)
        node_inputs = jnp.concatenate([flat_rows, summed.astype(jnp.bfloat16)], axis=1)
        node_delta, node_saved = mlp_forward(node_inputs, node_hidden[depth_index], node_offset[depth_index], node_output[depth_index], node_scale[depth_index])
        state = to_grid((flat_rows.astype(jnp.float32) + node_delta).astype(jnp.bfloat16).reshape(DEVICES, NODE_DEV, D))
        records.append((edge_saved, node_saved))
    node_result = state
    grad_grid = output_cotangent.astype(jnp.float32)
    grad_edges = jnp.zeros((DEVICES, EDGE_DEV, D), jnp.float32)
    per_layer = [None] * LAYERS
    for depth_index in reversed(range(LAYERS)):
        edge_saved, node_saved = records[depth_index]
        grad_rows = to_devices(grad_grid).reshape(-1, D)
        grad_in, node_grads = mlp_backward(grad_rows, node_saved, node_hidden[depth_index], node_output[depth_index], node_scale[depth_index])
        grad_rows = grad_rows + grad_in[:, :D]
        flow_grad = (grad_in[:, D:][recv_ids].reshape(DEVICES, EDGE_DEV, D) + grad_edges) * live_mask
        grad_inputs, edge_grads = mlp_backward(flow_grad.reshape(-1, D), edge_saved, edge_hidden[depth_index], edge_output[depth_index], edge_scale[depth_index])
        grad_inputs = grad_inputs.reshape(DEVICES, EDGE_DEV, 3 * D)
        grad_edges = grad_edges + grad_inputs[:, :, :D]
        grad_rows = grad_rows + jax.ops.segment_sum(grad_inputs[:, :, 2 * D:].reshape(-1, D), recv_ids, num_segments=DEVICES * NODE_DEV)
        table_grad = jax.ops.segment_sum(grad_inputs[:, :, D:2 * D].reshape(-1, D), send_ids, num_segments=DEVICES * (EXT + COARSE)).reshape(DEVICES, EXT + COARSE, D)
        grad_grid = to_grid(grad_rows.reshape(DEVICES, NODE_DEV, D)) + fold_blocks(table_grad[:, :EXT]) + coarse_into_grid(lax.optimization_barrier(jnp.sum(table_grad[:, EXT:], axis=0)))
        per_layer[depth_index] = edge_grads + node_grads
    factor = 1.0 / math.sqrt(NODES)
    stacked = [jnp.stack([per_layer[depth_index][item] for depth_index in range(LAYERS)]) * factor for item in range(8)]
    return (node_result, grad_grid, grad_edges, stacked[0], stacked[1], stacked[2], stacked[3], stacked[4], stacked[5], stacked[6], stacked[7])
```

```python
import math

import jax
import jax.numpy as jnp
from jax import lax
from jax.sharding import PartitionSpec as P

CO = 2
PIECES = 32
EPSILON = 1e-05
F32 = jnp.float32
BF16 = jnp.bfloat16


def moved(value, axis, by):
    count = lax.axis_size(axis)
    return lax.ppermute(value, axis, [(i, (i + by) % count) for i in range(count)])


def swapped(value, stage):
    axis, bit = stage
    return lax.ppermute(value, axis, [(i, i ^ bit) for i in range(lax.axis_size(axis))])


def axis_bits(axis):
    return [(axis, 1 << k) for k in range(lax.axis_size(axis).bit_length() - 1)]


def added(first, second):
    return (first.astype(F32) + second.astype(F32)).astype(BF16)


def scatter_sum(pieces, order):
    half = pieces.shape[0] // 2
    keep, send = pieces[:half], pieces[half:]
    for step, stage in enumerate(order):
        recv = swapped(send, stage)
        if half == 1:
            return added(keep, recv)
        half //= 2
        send = added(keep[half:], recv[half:])
        keep = added(keep[:half], recv[:half])


def gathered(piece, order):
    for stage in reversed(order):
        piece = jnp.concatenate([piece, swapped(piece, stage)], axis=0)
    return piece


def stage_orders():
    sector, band = axis_bits("sector"), axis_bits("band")
    depth = PIECES.bit_length() - 1
    first = sector + band
    second = sector[:1] + sector[1:][::-1] + band
    return (first[:depth], second[:depth]), first[depth:]


def summed_pieces(pieces):
    orders, rest = stage_orders()
    outs = []
    for part, order in enumerate(orders):
        own = scatter_sum(pieces[part], order)
        for stage in rest:
            own = added(own, swapped(own, stage))
        outs.append(gathered(own, order))
    return outs


def relative_index():
    orders, _ = stage_orders()
    table = []
    for order in orders:
        index = jnp.zeros((PIECES,), jnp.int32)
        span = PIECES
        for k, (axis, bit) in enumerate(order):
            span //= 2
            own = (lax.axis_index(axis) // bit) % 2
            position = (jnp.arange(PIECES, dtype=jnp.int32) // span) % 2
            index = index + (own ^ position) * span
        table.append(index)
    return table


def summed_vectors(values):
    for stage in axis_bits("sector") + axis_bits("band"):
        values = values + swapped(values, stage)
    return values


def sender_rows(senders, lat, lon, payload, own_rows):
    bands, sectors = lax.axis_size("band"), lax.axis_size("sector")
    width = lon + 2 * lat
    ext = 3 * lat * width
    row, col = senders // width, senders % width
    block, row = row // lat, row % lat
    base = jnp.where(block == 1, 0, jnp.where(block == 0, payload, 2 * payload))
    rim = lat * lat
    inside = jnp.where(
        col < lat,
        own_rows + row * lat + col,
        jnp.where(col < lat + lon, row * lon + col - lat, own_rows + rim + row * lat + col - lat - lon),
    )
    coarse = senders - ext
    owner, item = coarse // CO, coarse % CO
    away = (owner // sectors - lax.axis_index("band") + bands) % bands
    spot = (owner % sectors) * CO + item
    head = own_rows + 2 * rim
    coarse_row = jnp.where(
        away == 0,
        head + spot,
        jnp.where(
            away == bands - 1,
            payload + head + spot,
            jnp.where(away == 1, 2 * payload + head + spot, 3 * payload + (away - 2) * sectors * CO + spot),
        ),
    )
    return jnp.where(senders < ext, base + inside, coarse_row)


def collected(state, lat, lon):
    width = state.shape[-1]
    grid = state.reshape(lat, lon, width)
    sectors, bands = lax.axis_size("sector"), lax.axis_size("band")
    here = lax.axis_index("sector")
    rims = jnp.concatenate([grid[:, :lat], grid[:, lon - lat :]], axis=1)
    around = lax.all_gather(rims, "sector")
    west = lax.dynamic_index_in_dim(around, (here + sectors - 1) % sectors, 0, False)[:, lat:]
    east = lax.dynamic_index_in_dim(around, (here + 1) % sectors, 0, False)[:, :lat]
    coarse = around[:, 0, :CO].reshape(sectors * CO, width)
    payload = jnp.concatenate(
        [state, west.reshape(lat * lat, width), east.reshape(lat * lat, width), coarse], axis=0
    )
    north = moved(payload, "band", 1)
    south = moved(payload, "band", -1)
    others = [moved(coarse, "band", -away) for away in range(2, bands - 1)]
    return jnp.concatenate([payload, north, south] + others, axis=0)


def returned(table_grad, lat, lon, payload):
    width = table_grad.shape[-1]
    sectors, bands = lax.axis_size("sector"), lax.axis_size("band")
    own_rows, rim = lat * lon, lat * lat
    low = table_grad[payload:].astype(BF16)
    head = own_rows + 2 * rim
    from_south = moved(low[:payload], "band", -1)
    from_north = moved(low[payload : 2 * payload], "band", 1)
    total = table_grad[:payload] + from_south.astype(F32) + from_north.astype(F32)
    coarse = total[head:]
    for away in range(2, bands - 1):
        start = 2 * payload + (away - 2) * sectors * CO
        coarse = coarse + moved(low[start : start + sectors * CO], "band", away).astype(F32)
    rims = total[own_rows:head].astype(BF16)
    from_east = moved(rims[:rim], "sector", -1).astype(F32).reshape(lat, lat, width)
    from_west = moved(rims[rim:], "sector", 1).astype(F32).reshape(lat, lat, width)
    spread = lax.all_to_all(
        coarse.astype(BF16).reshape(sectors, CO, width), "sector", 0, 0, tiled=True
    )
    mine = jnp.sum(spread.astype(F32), axis=0)
    grid = total[:own_rows].reshape(lat, lon, width)
    grid = grid.at[:, lon - lat :].add(from_east).at[:, :lat].add(from_west)
    return grid.reshape(own_rows, width).at[:CO].add(mine)


def mlp_forward(inputs, first_weight, first_bias, second_weight, norm_gain):
    pre_act = jnp.dot(inputs, first_weight, preferred_element_type=F32) + first_bias
    sigmoid_val = jax.nn.sigmoid(pre_act)
    activated = (pre_act * sigmoid_val).astype(BF16)
    mixed = jnp.dot(activated, second_weight, preferred_element_type=F32)
    centered = mixed - jnp.mean(mixed, axis=-1, keepdims=True)
    inv_std = lax.rsqrt(jnp.mean(centered * centered, axis=-1, keepdims=True) + EPSILON)
    normed = centered * inv_std
    return (normed * norm_gain, (inputs, pre_act, sigmoid_val, activated, normed, inv_std))


def mlp_backward(grad_out, saved, first_weight, second_weight, norm_gain):
    inputs, pre_act, sigmoid_val, activated, normed, inv_std = saved
    grad_gain = jnp.sum(grad_out * normed, axis=0)
    grad_normed = grad_out * norm_gain
    grad_mixed = inv_std * (
        grad_normed
        - jnp.mean(grad_normed, axis=-1, keepdims=True)
        - normed * jnp.mean(grad_normed * normed, axis=-1, keepdims=True)
    )
    mixed_low = grad_mixed.astype(BF16)
    grad_second = lax.dot_general(
        activated, mixed_low, (((0,), (0,)), ((), ())), preferred_element_type=F32
    )
    grad_act = lax.dot_general(
        mixed_low, second_weight, (((1,), (1,)), ((), ())), preferred_element_type=F32
    )
    grad_pre = grad_act * sigmoid_val * (1.0 + pre_act * (1.0 - sigmoid_val))
    grad_bias = jnp.sum(grad_pre, axis=0)
    pre_low = grad_pre.astype(BF16)
    grad_first = lax.dot_general(
        inputs, pre_low, (((0,), (0,)), ((), ())), preferred_element_type=F32
    )
    grad_inputs = lax.dot_general(
        pre_low, first_weight, (((1,), (1,)), ((), ())), preferred_element_type=F32
    )
    return (grad_inputs, (grad_first, grad_bias, grad_second, grad_gain))


def picked(onehot, rows, transpose=False):
    dims = (((0,), (0,)), ((), ())) if transpose else (((1,), (0,)), ((), ()))
    high = rows.astype(BF16)
    low = (rows - high.astype(F32)).astype(BF16)
    out = lax.dot_general(onehot, high, dims, preferred_element_type=F32)
    return out + lax.dot_general(onehot, low, dims, preferred_element_type=F32)


def local(
    node_states,
    edge_states,
    senders,
    receivers,
    edge_count,
    edge_hidden,
    edge_offset,
    edge_output,
    edge_scale,
    node_hidden,
    node_offset,
    node_output,
    node_scale,
    output_cotangent,
):
    lat, lon, width = node_states.shape
    own_rows = lat * lon
    slots = edge_states.shape[1]
    depth = edge_hidden.shape[0]
    sectors, bands = lax.axis_size("sector"), lax.axis_size("band")
    payload = own_rows + 2 * lat * lat + sectors * CO
    table_rows = 3 * payload + (bands - 3) * sectors * CO
    edge_rows = edge_states[0]
    recv_index = receivers[0]
    send_index = sender_rows(senders[0], lat, lon, payload, own_rows)
    live_mask = (jnp.arange(slots, dtype=jnp.int32) < edge_count[0]).astype(F32)[:, None]
    incidence = (recv_index[:, None] == jnp.arange(own_rows, dtype=jnp.int32)[None, :]).astype(BF16)
    sender_onehot = (
        send_index[:, None] == jnp.arange(table_rows, dtype=jnp.int32)[None, :]
    ).astype(BF16)
    state = node_states.reshape(own_rows, width)
    records = []
    for step in range(depth):
        table = collected(state, lat, lon)
        sent = jnp.dot(sender_onehot, table, preferred_element_type=F32).astype(BF16)
        received = jnp.dot(incidence, state, preferred_element_type=F32).astype(BF16)
        inputs = jnp.concatenate([edge_rows, sent, received], axis=1)
        result, edge_saved = mlp_forward(
            inputs, edge_hidden[step], edge_offset[step], edge_output[step], edge_scale[step]
        )
        update = result * live_mask
        total = picked(incidence, update, True)
        node_inputs = jnp.concatenate([state, total.astype(BF16)], axis=1)
        node_delta, node_saved = mlp_forward(
            node_inputs, node_hidden[step], node_offset[step], node_output[step], node_scale[step]
        )
        records.append((edge_saved, node_saved))
        edge_rows = (edge_rows.astype(F32) + update).astype(BF16)
        state = (state.astype(F32) + node_delta).astype(BF16)
    node_result = state.reshape(lat, lon, width)
    grad_state = output_cotangent.reshape(own_rows, width).astype(F32)
    grad_edges = jnp.zeros((slots, width), F32)
    vectors = [None] * depth
    sums = [None] * depth
    index = relative_index()
    for step in reversed(range(depth)):
        edge_saved, node_saved = records[step]
        grad_in, node_grads = mlp_backward(
            grad_state, node_saved, node_hidden[step], node_output[step], node_scale[step]
        )
        grad_state = grad_state + grad_in[:, :width]
        flow_grad = (picked(incidence, grad_in[:, width:]) + grad_edges) * live_mask
        grad_inputs, edge_grads = mlp_backward(
            flow_grad, edge_saved, edge_hidden[step], edge_output[step], edge_scale[step]
        )
        grad_edges = grad_edges + grad_inputs[:, :width]
        grad_state = grad_state + picked(incidence, grad_inputs[:, 2 * width :], True)
        table_grad = picked(sender_onehot, grad_inputs[:, width : 2 * width], True)
        grad_state = grad_state + returned(table_grad, lat, lon, payload)
        stacked = jnp.concatenate([edge_grads[0], edge_grads[2], node_grads[0], node_grads[2]], axis=0)
        stacked = stacked.astype(BF16).reshape(-1, PIECES, width // PIECES, width)
        stacked = jnp.moveaxis(stacked, 1, 0)
        half = width // 2
        parts = jnp.stack(
            [
                jnp.take(stacked[..., part * half : (part + 1) * half], index[part], axis=0)
                for part in range(2)
            ]
        )
        sums[step] = summed_pieces(parts)
        vectors[step] = jnp.stack([edge_grads[1], edge_grads[3], node_grads[1], node_grads[3]])
    vectors = summed_vectors(jnp.stack(vectors))
    factor = 1.0 / math.sqrt(own_rows * bands * sectors)
    matrices = []
    for step in range(depth):
        halves = [jnp.take(sums[step][part], index[part], axis=0) for part in range(2)]
        whole = jnp.concatenate(halves, axis=-1)
        whole = jnp.moveaxis(whole, 0, 1).reshape(-1, width).astype(F32) * factor
        matrices.append(whole)
    matrices = jnp.stack(matrices)
    vectors = vectors * factor
    return (
        node_result,
        grad_state.reshape(lat, lon, width),
        grad_edges[None],
        matrices[:, : 3 * width],
        vectors[:, 0],
        matrices[:, 3 * width : 4 * width],
        vectors[:, 1],
        matrices[:, 4 * width : 6 * width],
        vectors[:, 2],
        matrices[:, 6 * width :],
        vectors[:, 3],
    )


def solution(mesh):
    grid = P("band", "sector", None)
    edges = P(("band", "sector"), None, None)
    index = P(("band", "sector"), None)
    return jax.shard_map(
        local,
        mesh=mesh,
        in_specs=(grid, edges, index, index, P(("band", "sector"))) + (P(),) * 8 + (grid,),
        out_specs=(grid, grid, edges) + (P(),) * 8,
        check_vma=False,
    )
```

```python
import functools
import math

import jax
import jax.numpy as jnp
from jax import lax
from jax.experimental import pallas as pl
from jax.experimental.pallas import tpu as pltpu
from jax.sharding import PartitionSpec as P

CO = 2
PIECES = 32
BLOCK = 256
VMEM = pltpu.VMEM
EPSILON = 1e-05
F32 = jnp.float32
BF16 = jnp.bfloat16


def moved(value, axis, by):
    count = lax.axis_size(axis)
    return lax.ppermute(value, axis, [(i, (i + by) % count) for i in range(count)])


def swapped(value, stage):
    axis, bit = stage
    return lax.ppermute(value, axis, [(i, i ^ bit) for i in range(lax.axis_size(axis))])


def axis_bits(axis):
    return [(axis, 1 << k) for k in range(lax.axis_size(axis).bit_length() - 1)]


def added(first, second):
    return (first.astype(F32) + second.astype(F32)).astype(BF16)


def scatter_sum(pieces, order):
    half = pieces.shape[0] // 2
    keep, send = pieces[:half], pieces[half:]
    for step, stage in enumerate(order):
        recv = swapped(send, stage)
        if half == 1:
            return added(keep, recv)
        half //= 2
        send = added(keep[half:], recv[half:])
        keep = added(keep[:half], recv[:half])


def gathered(piece, order):
    for stage in reversed(order):
        piece = jnp.concatenate([piece, swapped(piece, stage)], axis=0)
    return piece


def stage_orders():
    sector, band = axis_bits("sector"), axis_bits("band")
    depth = PIECES.bit_length() - 1
    first = sector + band
    second = sector[:1] + sector[1:][::-1] + band
    return (first[:depth], second[:depth]), first[depth:]


def summed_pieces(pieces):
    orders, rest = stage_orders()
    outs = []
    for part, order in enumerate(orders):
        own = scatter_sum(pieces[part], order)
        for stage in rest:
            own = added(own, swapped(own, stage))
        outs.append(gathered(own, order))
    return outs


def piece_masks():
    orders, _ = stage_orders()
    masks = []
    for order in orders:
        mask, span = 0, PIECES
        for axis, bit in order:
            span //= 2
            mask = mask + ((lax.axis_index(axis) // bit) % 2) * span
        masks.append(mask)
    return masks


def whole():
    return pl.BlockSpec(memory_space=VMEM)


def layer(array, step):
    shape = array.shape[1:]
    return pl.BlockSpec((None,) + shape, lambda *_: (step,) + (0,) * len(shape))


def dot(first, second):
    return jnp.dot(first, second, preferred_element_type=F32)


def dot_rows(first, second):
    return lax.dot_general(first, second, (((0,), (0,)), ((), ())), preferred_element_type=F32)


def dot_columns(first, second):
    return lax.dot_general(first, second, (((1,), (1,)), ((), ())), preferred_element_type=F32)


def split(value):
    high = value.astype(BF16)
    return high, (value - high.astype(F32)).astype(BF16)


def ones_at(equal):
    return jnp.where(equal, 1.0, 0.0).astype(BF16)


def iota(shape, dim):
    return lax.broadcasted_iota(jnp.int32, shape, dim)


def quotient(value, divisor, limit):
    factor = -(-(1 << 18) // divisor)
    assert all((v * factor) >> 18 == v // divisor for v in range(limit))
    return (value * factor) >> 18


def index_kernel(lat, lon, payload, bands, sectors, senders, receivers, send_row, send_col, recv_col):
    own_rows, rim, width = lat * lon, lat * lat, lon + 2 * lat
    ext = 3 * lat * width
    limit = ext + CO * bands * sectors
    value = senders[...]
    row = quotient(value, width, limit)
    col = value - row * width
    block = quotient(row, lat, limit)
    row = row - block * lat
    base = jnp.where(block == 1, 0, jnp.where(block == 0, payload, 2 * payload))
    inside = jnp.where(
        col < lat,
        own_rows + row * lat + col,
        jnp.where(col < lat + lon, row * lon + col - lat, own_rows + rim + row * lat + col - lat - lon),
    )
    coarse = jnp.maximum(value - ext, 0)
    spots = sectors * CO
    band = quotient(coarse, spots, limit)
    spot = coarse - band * spots
    away = band - lax.axis_index("band")
    away = jnp.where(away < 0, away + bands, away)
    head = own_rows + 2 * rim
    coarse_row = jnp.where(
        away == 0,
        head + spot,
        jnp.where(
            away == bands - 1,
            payload + head + spot,
            jnp.where(away == 1, 2 * payload + head + spot, 3 * payload + (away - 2) * spots + spot),
        ),
    )
    result = jnp.where(value < ext, base + inside, coarse_row)
    send_row[...] = result
    slots = value.shape[1]
    send_col[...] = jnp.transpose(jnp.broadcast_to(result, (8, slots)))[:, :1]
    recv_col[...] = jnp.transpose(jnp.broadcast_to(receivers[...], (8, slots)))[:, :1]


def fill_table(table, parts):
    start = 0
    for part in parts:
        table[pl.ds(start, part.shape[0]), :] = part[...]
        start += part.shape[0]
    if start < table.shape[0]:
        table[pl.ds(start, table.shape[0] - start), :] = jnp.zeros(
            (table.shape[0] - start, table.shape[1]), BF16
        )


def activated(pre):
    sigmoid = jax.nn.sigmoid(pre)
    return sigmoid, (pre * sigmoid).astype(BF16)


def normalised(mixed):
    centered = mixed - jnp.mean(mixed, axis=-1, keepdims=True)
    inv_std = lax.rsqrt(jnp.mean(centered * centered, axis=-1, keepdims=True) + EPSILON)
    return centered * inv_std, inv_std


def forward_kernel(parts, own_rows, last, *refs):
    count, send_col, recv_col, recv_row, edges = refs[:5]
    table_parts = refs[5 : 5 + parts]
    w1, c1, w2, g1, v1, d1, v2, g2 = refs[5 + parts : 13 + parts]
    outs = refs[13 + parts : -2]
    table, total = refs[-2:]
    pre_out, norm_out, std_out, node_pre, node_norm, node_std, agg_out, state_out = outs[:8]
    width = w2.shape[1]
    block = pl.program_id(0)

    @pl.when(block == 0)
    def _():
        fill_table(table, table_parts)
        total[...] = jnp.zeros_like(total)

    state = table[pl.ds(0, own_rows), :]
    edge = edges[...]
    rows = edge.shape[0]
    sent = dot(ones_at(iota((rows, table.shape[0]), 1) == send_col[...]), table[...]).astype(BF16)
    received = dot(ones_at(iota((rows, own_rows), 1) == recv_col[...]), state).astype(BF16)
    pre = (
        dot(edge, w1[pl.ds(0, width), :])
        + dot(sent, w1[pl.ds(width, width), :])
        + dot(received, w1[pl.ds(2 * width, width), :])
        + c1[...]
    )
    _, act = activated(pre)
    normed, inv_std = normalised(dot(act, w2[...]))
    live = (iota((rows, 1), 0) + block * rows < count[0]).astype(F32)
    update = normed * g1[...] * live
    pre_out[...] = pre
    norm_out[...] = normed
    std_out[...] = inv_std
    high, low = split(update)
    reach = ones_at(iota((own_rows, rows), 0) == recv_row[...])
    total[...] += dot(reach, high) + dot(reach, low)
    if not last:
        outs[8][...] = (edge.astype(F32) + update).astype(BF16)

    @pl.when(block == pl.num_programs(0) - 1)
    def _():
        agg = total[...].astype(BF16)
        pre = dot(state, v1[pl.ds(0, width), :]) + dot(agg, v1[pl.ds(width, width), :]) + d1[...]
        _, act = activated(pre)
        normed, inv_std = normalised(dot(act, v2[...]))
        node_pre[...] = pre
        node_norm[...] = normed
        node_std[...] = inv_std
        agg_out[...] = agg
        state_out[...] = (state.astype(F32) + normed * g2[...]).astype(BF16)


def mlp_back(grad_out, pre, normed, inv_std, gain, second):
    grad_gain = jnp.sum(grad_out * normed, axis=0, keepdims=True)
    grad_normed = grad_out * gain
    mixed = inv_std * (
        grad_normed
        - jnp.mean(grad_normed, axis=-1, keepdims=True)
        - normed * jnp.mean(grad_normed * normed, axis=-1, keepdims=True)
    )
    mixed = mixed.astype(BF16)
    grad_act = dot_columns(mixed, second)
    sigmoid, act = activated(pre)
    grad_pre = grad_act * sigmoid * (1.0 + pre * (1.0 - sigmoid))
    grad_bias = jnp.sum(grad_pre, axis=0, keepdims=True)
    return act, mixed, grad_pre.astype(BF16), grad_bias, grad_gain


def backward_kernel(own_rows, payload, first, *refs):
    (count, send_row, recv_col, recv_row, grad_state) = refs[:5]
    pre, normed, std, node_pre, node_norm, node_std = refs[5:11]
    w1, w2, g1, v1, v2, g2 = refs[11:17]
    rest = refs[17:]
    if first:
        grad_edges, rest = None, rest
    else:
        grad_edges, rest = rest[0], rest[1:]
    (edge_act, edge_mixed, edge_low, node_act, node_mixed, node_low) = rest[:6]
    (by_sender, by_receiver, near, far, edges_out, vectors) = rest[6:12]
    sums, hubs, spread, bias, gain = rest[12:]
    width = w2.shape[1]
    block = pl.program_id(0)

    @pl.when(block == 0)
    def _():
        act, mixed, low, grad_bias, grad_gain = mlp_back(
            grad_state[...].astype(F32), node_pre[...], node_norm[...], node_std[...], g2[...], v2[...]
        )
        node_act[...], node_mixed[...], node_low[...] = act, mixed, low
        vectors[pl.ds(2, 1), :] = grad_bias
        vectors[pl.ds(3, 1), :] = grad_gain
        spread[...] = dot_columns(low, v1[pl.ds(width, width), :])
        sums[...] = jnp.zeros_like(sums)
        hubs[...] = jnp.zeros_like(hubs)
        bias[...] = jnp.zeros_like(bias)
        gain[...] = jnp.zeros_like(gain)

    rows = pre.shape[0]
    high, low = split(spread[...])
    reach = ones_at(iota((rows, own_rows), 1) == recv_col[...])
    flow = dot(reach, high) + dot(reach, low)
    if not first:
        flow = flow + grad_edges[...]
    flow = flow * (iota((rows, 1), 0) + block * rows < count[0]).astype(F32)
    act, mixed, pre_low, grad_bias, grad_gain = mlp_back(
        flow, pre[...], normed[...], std[...], g1[...], w2[...]
    )
    edge_act[...], edge_mixed[...], edge_low[...] = act, mixed, pre_low
    bias[...] += grad_bias
    gain[...] += grad_gain
    grad = dot_columns(pre_low, w1[pl.ds(0, width), :])
    edges_out[...] = grad if first else grad_edges[...] + grad
    sums[...] += dot(ones_at(iota((sums.shape[0], rows), 0) == send_row[...]), pre_low)
    hubs[...] += dot(ones_at(iota((own_rows, rows), 0) == recv_row[...]), pre_low)

    @pl.when(block == pl.num_programs(0) - 1)
    def _():
        sender_low = sums[...].astype(BF16)
        hub_low = hubs[...].astype(BF16)
        by_sender[...] = sender_low
        by_receiver[...] = hub_low
        table_grad = dot_columns(sender_low, w1[pl.ds(width, width), :])
        own = (
            grad_state[...].astype(F32)
            + dot_columns(node_low[...], v1[pl.ds(0, width), :])
            + dot_columns(hub_low, w1[pl.ds(2 * width, width), :])
        )
        near[pl.ds(0, own_rows), :] = own + table_grad[:own_rows]
        near[pl.ds(own_rows, payload - own_rows), :] = table_grad[own_rows:payload]
        far[...] = table_grad[payload : payload + far.shape[0]].astype(BF16)
        vectors[pl.ds(0, 1), :] = bias[...]
        vectors[pl.ds(1, 1), :] = gain[...]


def weights_kernel(parts, own_rows, *refs):
    edges = refs[0]
    table_parts = refs[1 : 1 + parts]
    (edge_act, edge_mixed, edge_low, node_act, node_mixed, node_low, by_sender, by_receiver, agg) = refs[
        1 + parts : 10 + parts
    ]
    out = refs[10 + parts : 12 + parts]
    table = refs[-1]
    fill_table(table, table_parts)
    masks = piece_masks()
    state = table[pl.ds(0, own_rows), :]
    pairs = [
        (edges[...], edge_low[...]),
        (table[...], by_sender[...]),
        (state, by_receiver[...]),
        (edge_act[...], edge_mixed[...]),
        (state, node_low[...]),
        (agg[...], node_low[...]),
        (node_act[...], node_mixed[...]),
    ]
    for slot, (left, right) in enumerate(pairs):
        grad = dot_rows(left, right).astype(BF16)
        rows, half = grad.shape[0] // PIECES, grad.shape[1] // 2
        for piece in range(PIECES):
            for part in range(2):
                out[part][piece ^ masks[part], slot] = grad[
                    piece * rows : (piece + 1) * rows, part * half : (part + 1) * half
                ]


def results_kernel(step, factor, given, *refs):
    sums = refs[:2]
    vectors = refs[2]
    refs = refs[3 + given :]
    outs, vector_outs = refs[:4], refs[4:-2]
    stage, done = refs[-2:]
    masks = piece_masks()
    width = stage.shape[-1]
    copies = []
    slot = 0
    for out in outs:
        for part in range(out.shape[1] // width):
            rows, half = width // PIECES, width // 2
            for piece in range(PIECES):
                for side in range(2):
                    stage[slot, pl.ds(piece * rows, rows), pl.ds(side * half, half)] = (
                        sums[side][piece ^ masks[side], slot].astype(F32) * factor
                    )
            copy = pltpu.make_async_copy(
                stage.at[slot], out.at[step, pl.ds(part * width, width), :], done.at[slot]
            )
            copy.start()
            copies.append(copy)
            slot += 1
    for item, out in enumerate(vector_outs):
        out[...] = vectors[:, item] * factor
    for copy in copies:
        copy.wait()


def summed_vectors(values):
    for stage in axis_bits("sector") + axis_bits("band"):
        values = values + swapped(values, stage)
    return values


def collected(state, lat, lon):
    width = state.shape[-1]
    grid = state.reshape(lat, lon, width)
    sectors, bands = lax.axis_size("sector"), lax.axis_size("band")
    here = lax.axis_index("sector")
    rims = jnp.concatenate([grid[:, :lat], grid[:, lon - lat :]], axis=1)
    around = lax.all_gather(rims, "sector")
    west = lax.dynamic_index_in_dim(around, (here + sectors - 1) % sectors, 0, False)[:, lat:]
    east = lax.dynamic_index_in_dim(around, (here + 1) % sectors, 0, False)[:, :lat]
    coarse = around[:, 0, :CO].reshape(sectors * CO, width)
    payload = jnp.concatenate(
        [state, west.reshape(lat * lat, width), east.reshape(lat * lat, width), coarse], axis=0
    )
    north = moved(payload, "band", 1)
    south = moved(payload, "band", -1)
    others = [moved(coarse, "band", -away) for away in range(2, bands - 1)]
    return [payload, north, south] + others


def returned(near, low, lat, lon, payload):
    width = near.shape[-1]
    sectors, bands = lax.axis_size("sector"), lax.axis_size("band")
    own_rows, rim = lat * lon, lat * lat
    head = own_rows + 2 * rim
    from_south = moved(low[:payload], "band", -1)
    from_north = moved(low[payload : 2 * payload], "band", 1)
    total = near + from_south.astype(F32) + from_north.astype(F32)
    coarse = total[head:]
    for away in range(2, bands - 1):
        start = 2 * payload + (away - 2) * sectors * CO
        coarse = coarse + moved(low[start : start + sectors * CO], "band", away).astype(F32)
    rims = total[own_rows:head].astype(BF16)
    from_east = moved(rims[:rim], "sector", -1).astype(F32).reshape(lat, lat, width)
    from_west = moved(rims[rim:], "sector", 1).astype(F32).reshape(lat, lat, width)
    spread = lax.all_to_all(
        coarse.astype(BF16).reshape(sectors, CO, width), "sector", 0, 0, tiled=True
    )
    mine = jnp.sum(spread.astype(F32), axis=0)
    grid = total[:own_rows].reshape(lat, lon, width)
    grid = grid.at[:, lon - lat :].add(from_east).at[:, :lat].add(from_west)
    return grid.reshape(own_rows, width).at[:CO].add(mine)


def local(
    node_states,
    edge_states,
    senders,
    receivers,
    edge_count,
    edge_hidden,
    edge_offset,
    edge_output,
    edge_scale,
    node_hidden,
    node_offset,
    node_output,
    node_scale,
    output_cotangent,
):
    lat, lon, width = node_states.shape
    own_rows = lat * lon
    slots = edge_states.shape[1]
    depth = edge_hidden.shape[0]
    sectors, bands = lax.axis_size("sector"), lax.axis_size("band")
    payload = own_rows + 2 * lat * lat + sectors * CO
    table_rows = 3 * payload + (bands - 3) * sectors * CO
    padded = -(-table_rows // 128) * 128
    blocks = slots // BLOCK
    shape = jax.ShapeDtypeStruct
    row_vectors = [v[:, None] for v in (edge_offset, edge_scale, node_offset, node_scale)]
    c1, g1, d1, g2 = row_vectors

    send_row, send_col, recv_col = pl.pallas_call(
        functools.partial(index_kernel, lat, lon, payload, bands, sectors),
        out_shape=(shape((1, slots), jnp.int32), shape((slots, 1), jnp.int32), shape((slots, 1), jnp.int32)),
        name="index",
    )(senders, receivers)

    smem = pl.BlockSpec(memory_space=pltpu.SMEM)
    by_rows = pl.BlockSpec((BLOCK, width), lambda i: (i, 0))
    by_col = pl.BlockSpec((BLOCK, 1), lambda i: (i, 0))
    by_row = pl.BlockSpec((1, BLOCK), lambda i: (0, i))

    def fixed(*dims):
        return pl.BlockSpec(dims, lambda i: (0,) * len(dims))

    unit = slots * width * width * 2
    state = node_states.reshape(own_rows, width)
    edge_rows = edge_states[0]
    records = []
    for step in range(depth):
        last = step == depth - 1
        parts = collected(state, lat, lon)
        out_shape = [
            shape((slots, width), F32),
            shape((slots, width), F32),
            shape((slots, 1), F32),
            shape((own_rows, width), F32),
            shape((own_rows, width), F32),
            shape((own_rows, 1), F32),
            shape((own_rows, width), BF16),
            shape((own_rows, width), BF16),
        ] + ([] if last else [shape((slots, width), BF16)])
        wide, thin = fixed(own_rows, width), fixed(own_rows, 1)
        out_specs = [by_rows, by_rows, by_col, wide, wide, thin, wide, wide] + ([] if last else [by_rows])
        weights = (edge_hidden, c1, edge_output, g1, node_hidden, d1, node_output, g2)
        outs = pl.pallas_call(
            functools.partial(forward_kernel, len(parts), own_rows, last),
            grid=(blocks,),
            out_shape=out_shape,
            in_specs=[smem, by_col, by_col, by_row, by_rows]
            + [fixed(*p.shape) for p in parts]
            + [layer(w, step) for w in weights],
            out_specs=out_specs,
            scratch_shapes=[VMEM((padded, width), BF16), VMEM((own_rows, width), F32)],
            cost_estimate=pl.CostEstimate(flops=6 * unit, bytes_accessed=8 << 20, transcendentals=slots * width),
            name="forward",
        )(edge_count, send_col, recv_col, receivers, edge_rows, *parts, *weights)
        records.append((edge_rows, parts, outs))
        state = outs[7]
        if not last:
            edge_rows = outs[8]
    node_result = state.reshape(lat, lon, width)
    grad_state = output_cotangent.reshape(own_rows, width)
    grad_edges = None
    vectors = [None] * depth
    factor = 1.0 / math.sqrt(own_rows * bands * sectors)
    sums = [None] * depth
    for step in reversed(range(depth)):
        first = grad_edges is None
        edge_rows, parts, outs = records[step]
        pre, normed, std, node_pre, node_norm, node_std, agg = outs[:7]
        wide, thin = fixed(own_rows, width), fixed(own_rows, 1)
        weights = (edge_hidden, edge_output, g1, node_hidden, node_output, g2)
        acts = pl.pallas_call(
            functools.partial(backward_kernel, own_rows, payload, first),
            grid=(blocks,),
            in_specs=[smem, by_row, by_col, by_row, wide, by_rows, by_rows, by_col, wide, wide, thin]
            + [layer(w, step) for w in weights]
            + ([] if first else [by_rows]),
            out_shape=[shape((slots, width), BF16)] * 3
            + [shape((own_rows, width), BF16)] * 3
            + [
                shape((padded, width), BF16),
                shape((own_rows, width), BF16),
                shape((payload, width), F32),
                shape((table_rows - payload, width), BF16),
                shape((slots, width), F32),
                shape((4, width), F32),
            ],
            out_specs=[by_rows] * 3
            + [wide] * 3
            + [
                fixed(padded, width),
                wide,
                fixed(payload, width),
                fixed(table_rows - payload, width),
                by_rows,
                fixed(4, width),
            ],
            scratch_shapes=[
                VMEM((padded, width), F32),
                VMEM((own_rows, width), F32),
                VMEM((own_rows, width), F32),
                VMEM((1, width), F32),
                VMEM((1, width), F32),
            ],
            cost_estimate=pl.CostEstimate(flops=8 * unit, bytes_accessed=10 << 20, transcendentals=slots * width),
            name="backward",
        )(
            edge_count, send_row, recv_col, receivers, grad_state, pre, normed, std, node_pre, node_norm,
            node_std, *weights, *([] if first else [grad_edges])
        )
        grad_edges = acts[10]
        vectors[step] = acts[11]
        grad_state = returned(acts[8], acts[9], lat, lon, payload)
        slots7 = (edge_hidden.shape[1] + edge_output.shape[1] + node_hidden.shape[1] + node_output.shape[1]) // width
        piece = shape((PIECES, slots7, width // PIECES, width // 2), BF16)
        pieces = pl.pallas_call(
            functools.partial(weights_kernel, len(parts), own_rows),
            out_shape=(piece, piece),
            scratch_shapes=[VMEM((padded, width), BF16)],
            cost_estimate=pl.CostEstimate(flops=6 * unit, bytes_accessed=10 << 20, transcendentals=0),
            name="weights",
        )(edge_rows, *parts, *acts[:8], agg)
        sums[step] = summed_pieces(pieces)
    total = summed_vectors(jnp.stack(vectors))
    given = []
    for step in reversed(range(depth)):
        final = step == 0
        anywhere = pl.BlockSpec(memory_space=pl.ANY)
        arrays = (edge_hidden, edge_output, node_hidden, node_output)
        outs = pl.pallas_call(
            functools.partial(results_kernel, step, factor, len(given)),
            in_specs=[whole()] * 3 + [anywhere] * len(given),
            out_shape=[shape(a.shape, F32) for a in arrays] + ([shape((depth, width), F32)] * 4 if final else []),
            out_specs=[anywhere] * 4 + ([whole()] * 4 if final else []),
            input_output_aliases={3 + k: k for k in range(len(given))},
            scratch_shapes=[VMEM((slots7, width, width), F32), pltpu.SemaphoreType.DMA((slots7,))],
            cost_estimate=pl.CostEstimate(flops=1 << 20, bytes_accessed=8 << 20, transcendentals=0),
            name="results",
        )(*sums[step], total if final else vectors[step][None], *given)
        given = list(outs[:4])
    return (
        node_result,
        grad_state.reshape(lat, lon, width),
        grad_edges[None],
        outs[0],
        outs[4],
        outs[1],
        outs[5],
        outs[2],
        outs[6],
        outs[3],
        outs[7],
    )


def solution(mesh):
    grid = P("band", "sector", None)
    edges = P(("band", "sector"), None, None)
    index = P(("band", "sector"), None)
    return jax.shard_map(
        local,
        mesh=mesh,
        in_specs=(grid, edges, index, index, P(("band", "sector"))) + (P(),) * 8 + (grid,),
        out_specs=(grid, grid, edges) + (P(),) * 8,
        check_vma=False,
    )
```
